32 devices in a mesh: seq: 16 (over z, y, core), head: 2 (over x).
Axes of the slice: x: 2, y: 2, z: 4, core: 2. Of those that a mesh axis runs over, the one named last changes fastest.
Arguments:
- latents: bfloat16 [4096, 1024], P('seq', 'head'), may hold values from -6 to 6
- known: bfloat16 [4096, 1024], P('seq', 'head'), may hold values from -6 to 6
- seam_mask: int32 [4096], P('seq'), may hold values 0 or 1
- timesteps: int32 [3], replicated, may hold values from 302 to 800, as said below
- block_lists: int32 [32, 6], P('seq'), may hold values from -1 to 31, as said below
- guidance: bfloat16 [2, 128, 1024], P(None, 'seq'), may hold values from -7 to 7
- modulation_weight: bfloat16 [256, 4, 1024], replicated, may hold values from -0.75 to 0.75
- self_weight: bfloat16 [1024, 3, 1024], P(None, None, 'head')
- self_out_weight: bfloat16 [1024, 1024], P('head'), may hold values from -0.1875 to 0.1875
- cross_weight: bfloat16 [1024, 3, 1024], P(None, None, 'head')
- cross_out_weight: bfloat16 [1024, 1024], P('head'), may hold values from -0.1875 to 0.1875
Outputs:
- denoised: bfloat16 [4096, 1024], P('seq', 'head')
The draws below stay inside these ranges and needn't reach their ends.
Inputs may be any that keep to these rules, and one draw needn't show every extreme that they name: `block_lists`: row b starts with b itself, followed by distinct blocks of the query's own tile or of the tiles 1 and 4 away on either side along the closed band of 16 tiles; the rest of the row is -1. Some rows hold 6 blocks. `timesteps`: strictly falling.
All inputs are finite; a program needn't handle non-finite values. No bound on the sum of `seam_mask` on one device may be relied on, other than what follows from the above.
Results may differ from the reference program's by a relative error of at most 0.011.
Values may be sent and summed in bfloat16 or wider, within the bound.
No kernel may reach another device: no remote copies, remote signals or barrier semaphores. Data moves between devices by JAX's collectives and lax.ppermute only.
A program may use at most 128 MiB of HBM per device.

```python
import math
import jax
import jax.numpy as jnp
from jax import lax

D = 1024
HEADS = 16
HEAD_DIM = 64
FREQ = 256
BLOCK = 128
MAXK = 6
ROW = 4
STEPS = 2
TOK_DEV = 256
TOKENS = 4096
NBLK = 32
G = 128


def latent_base(key):
    fresh = jax.random.normal(jax.random.fold_in(key, 11), (TOKENS, D), jnp.float32)
    return jnp.clip(fresh, -6.0, 6.0)


def draw_latents(key, part):
    return latent_base(key).astype(jnp.bfloat16)


def draw_guidance(key, part):
    fresh = jnp.clip(jax.random.normal(jax.random.fold_in(key, 12), (STEPS, G, D), jnp.float32), -6.0, 6.0)
    stride = TOKENS // G
    copied = jnp.roll(latent_base(key)[::stride], G // 2, axis=0)
    result = copied[None, :, :] + 0.5 * fresh
    return jnp.clip(result, -7.0, 7.0).astype(jnp.bfloat16)


def projection(key, salt, aligned):
    base = jax.random.normal(jax.random.fold_in(key, salt), (D, 3, D), jnp.float32) / math.sqrt(D)
    query_part = 2.0 * base[:, 0]
    if aligned:
        key_part = query_part + 0.3 * base[:, 1]
    else:
        key_part = base[:, 1]
    return jnp.stack([query_part, key_part, base[:, 2]], axis=1).astype(jnp.bfloat16)


def draw_self_weight(key, part):
    return projection(key, 31, False)


def draw_cross_weight(key, part):
    return projection(key, 41, True)


def draw_timesteps(key, part):
    start = jnp.full((1,), 800, jnp.int32)
    gaps = jax.random.randint(jax.random.fold_in(key, 52), (STEPS,), 50, 250)
    return jnp.concatenate([start, start - jnp.cumsum(gaps)]).astype(jnp.int32)


def draw_block_lists(key, part):
    per_tile = TOK_DEV // BLOCK
    tiles = NBLK // per_tile
    block = jnp.arange(NBLK, dtype=jnp.int32)
    tile = block // per_tile
    moves = jnp.array([0, -1, 1, -ROW, ROW], dtype=jnp.int32)
    target = (tile[:, None] + moves[None, :]) % tiles
    within = jnp.arange(per_tile, dtype=jnp.int32)
    candidate = (target[:, :, None] * per_tile + within[None, None, :]).reshape(NBLK, 5 * per_tile)
    is_own = candidate == block[:, None]
    ranking = jax.random.randint(jax.random.fold_in(key, 61), (NBLK, 5 * per_tile), 0, 1 << 20) * 128
    ranking = ranking + jnp.arange(5 * per_tile, dtype=jnp.int32)[None, :]
    ranking = jnp.where(is_own, 1 << 28, ranking)
    order = jnp.argsort(ranking, axis=1)
    others = jnp.take_along_axis(candidate, order, axis=1)[:, :MAXK - 1]
    heat = jax.random.randint(jax.random.fold_in(key, 62), (tiles,), 0, 4)
    chosen_tile = jax.random.randint(jax.random.fold_in(key, 63), (), 0, tiles)
    hot_tile = (heat == 0) | (jnp.arange(tiles, dtype=jnp.int32) == chosen_tile)
    count = 1 + jax.random.randint(jax.random.fold_in(key, 64), (NBLK,), 0, MAXK - 1)
    count = jnp.where(hot_tile[tile], MAXK, count)
    listed = jnp.concatenate([block[:, None], others], axis=1)
    column = jnp.arange(MAXK, dtype=jnp.int32)[None, :]
    return jnp.where(column < count[:, None], listed, -1).astype(jnp.int32)


def touch_ends(values, stream_key, least, high):
    dims = values.shape
    index_at = [jax.random.randint(jax.random.fold_in(stream_key, axis), (), 0, dims[axis]) for axis in range(len(dims))]
    values = values.at[tuple(index_at)].set(least)
    longest = dims.index(max(dims))
    index_at[longest] = (index_at[longest] + 1) % dims[longest]
    return values.at[tuple(index_at)].set(high)


def shard_levels(stream_key, dims, pieces, smallest, largest):
    gain, own = 1.0, jax.random.fold_in(stream_key, 6)
    for position, parts in pieces:
        draws = jnp.exp(jax.random.uniform(jax.random.fold_in(own, position), (parts,), jnp.float32, smallest / len(pieces), largest / len(pieces)))
        gain = gain * jnp.repeat(draws, dims[position] // parts).reshape([-1 if axis == position else 1 for axis in range(len(dims))])
    return gain


def normal_values(stream_key, shape, spread, bound, cuts=(), held_as=jnp.bfloat16):
    factor_of = shard_levels(stream_key, shape, cuts, -0.22, 0.18) if cuts else 1.0
    values = jax.random.normal(stream_key, shape, jnp.float32) * spread * factor_of
    return jnp.minimum(jnp.maximum(values, -bound), bound).astype(held_as)


def setup_inputs(seed: int = 0) -> dict:
    keys = jax.random.split(jax.random.key(seed), 12)
    return {
        "latents": draw_latents(jax.random.fold_in(keys[11], 71), 0),
        "known": normal_values(keys[1], (TOKENS, D), 1.0, 6.0, ((0, 16), (1, 2))),
        "seam_mask": touch_ends((jax.random.randint(keys[2], (TOKENS,), 0, 2) < 1).astype(jnp.int32), jax.random.fold_in(keys[2], 1), 0, 1),
        "timesteps": draw_timesteps(jax.random.fold_in(keys[11], 71), 0),
        "block_lists": draw_block_lists(jax.random.fold_in(keys[11], 71), 0),
        "guidance": draw_guidance(jax.random.fold_in(keys[11], 71), 0),
        "modulation_weight": normal_values(keys[6], (FREQ, 4, D), (FREQ // 4) ** -0.5, 0.75),
        "self_weight": draw_self_weight(jax.random.fold_in(keys[11], 71), 0),
        "self_out_weight": normal_values(keys[8], (D, D), D ** -0.5, 0.1875, ((0, 2),)),
        "cross_weight": draw_cross_weight(jax.random.fold_in(keys[11], 71), 0),
        "cross_out_weight": normal_values(keys[10], (D, D), D ** -0.5, 0.1875, ((0, 2),)),
    }


def widen(values):
    return lax.optimization_barrier(values).astype(jnp.float32)

def norm_rows(values):
    values = values.astype(jnp.float32)
    center = values - lax.optimization_barrier(jnp.mean(values, axis=-1, keepdims=True))
    second = lax.optimization_barrier(jnp.mean(center * center, axis=-1, keepdims=True))
    return center * lax.rsqrt(second + 1e-06)

def signal_level(moment):
    angle = (moment.astype(jnp.float32) / 1000.0 + 0.008) / 1.008 * (math.pi / 2.0)
    cosine = jnp.cos(angle)
    return cosine * cosine

def modulation_table(moment, modulation_weight):
    half = FREQ // 2
    frequency = jnp.exp(-math.log(10000.0) * jnp.arange(half, dtype=jnp.float32) / half)
    phase = moment.astype(jnp.float32) * frequency
    embed = jnp.concatenate([jnp.cos(phase), jnp.sin(phase)])
    active = jax.nn.silu(embed).astype(jnp.bfloat16)
    width = modulation_weight.shape[2]
    table = jnp.dot(active[None, :], modulation_weight.reshape(FREQ, 4 * width), preferred_element_type=jnp.float32)
    return table.reshape(4, width)

def sparse_attention(query, pair, block_lists):
    scale = 1.0 / math.sqrt(HEAD_DIM)
    query_blocks = query.reshape(NBLK, BLOCK, HEADS, HEAD_DIM)
    pair_blocks = pair.reshape(NBLK, BLOCK, 2, HEADS, HEAD_DIM)

    def one_block(operand):
        queries, entries = operand
        valid = entries >= 0
        picked = jnp.where(valid, entries, 0).astype(jnp.int32)
        chosen = pair_blocks[picked].reshape(MAXK * BLOCK, 2, HEADS, HEAD_DIM)
        scores = jnp.einsum('qhd,khd->hqk', widen(queries), widen(chosen[:, 0])) * scale
        live = jnp.repeat(valid, BLOCK)
        scores = jnp.where(live[None, None, :], scores, -1e+30)
        peak = lax.optimization_barrier(jnp.max(scores, axis=-1, keepdims=True))
        weights = jnp.exp(scores - peak)
        total = lax.optimization_barrier(jnp.sum(weights, axis=-1))
        rounded = weights.astype(jnp.bfloat16)
        mixed = jnp.einsum('hqk,khd->qhd', widen(rounded), widen(chosen[:, 1]))
        mixed = mixed / jnp.transpose(total)[:, :, None]
        return mixed.reshape(BLOCK, HEADS * HEAD_DIM).astype(jnp.bfloat16)
    result = lax.map(one_block, (query_blocks, block_lists))
    return result.reshape(NBLK * BLOCK, HEADS * HEAD_DIM)

def guided_attention(query, guide_pair):
    scale = 1.0 / math.sqrt(HEAD_DIM)
    guide_keys = widen(guide_pair[:, 0]).reshape(G, HEADS, HEAD_DIM)
    guide_values = widen(guide_pair[:, 1]).reshape(G, HEADS, HEAD_DIM)
    query_blocks = query.reshape(NBLK, BLOCK, HEADS, HEAD_DIM)

    def one_block(queries):
        scores = jnp.einsum('qhd,ghd->hqg', widen(queries), guide_keys) * scale
        peak = lax.optimization_barrier(jnp.max(scores, axis=-1, keepdims=True))
        weights = jnp.exp(scores - peak)
        total = lax.optimization_barrier(jnp.sum(weights, axis=-1))
        rounded = weights.astype(jnp.bfloat16)
        mixed = jnp.einsum('hqg,ghd->qhd', widen(rounded), guide_values)
        mixed = mixed / jnp.transpose(total)[:, :, None]
        return mixed.reshape(BLOCK, HEADS * HEAD_DIM).astype(jnp.bfloat16)
    result = lax.map(one_block, query_blocks)
    return result.reshape(NBLK * BLOCK, HEADS * HEAD_DIM)

def reference(latents, known, seam_mask, timesteps, block_lists, guidance, modulation_weight, self_weight, self_out_weight, cross_weight, cross_out_weight):
    state = latents
    self_flat = self_weight.reshape(D, 3 * D)
    cross_pair_weight = cross_weight[:, 1:3].reshape(D, 2 * D)
    cross_query_weight = cross_weight[:, 0]
    for step in range(STEPS):
        moment = timesteps[step]
        after = timesteps[step + 1]
        table = modulation_table(moment, modulation_weight)
        normed = norm_rows(state)
        mixed_in = (normed * (1.0 + table[1]) + table[0]).astype(jnp.bfloat16)
        plain = normed.astype(jnp.bfloat16)
        projected = jnp.dot(mixed_in, self_flat, preferred_element_type=jnp.float32).astype(jnp.bfloat16)
        projected = projected.reshape(TOKENS, 3, D)
        attended = sparse_attention(projected[:, 0], projected[:, 1:3], block_lists)
        guide_in = norm_rows(guidance[step]).astype(jnp.bfloat16)
        guide_pair = jnp.dot(guide_in, cross_pair_weight, preferred_element_type=jnp.float32).astype(jnp.bfloat16)
        guide_pair = guide_pair.reshape(G, 2, D)
        cross_query = jnp.dot(plain, cross_query_weight, preferred_element_type=jnp.float32).astype(jnp.bfloat16)
        guided = guided_attention(cross_query, guide_pair)
        noise_pred = table[2] * jnp.dot(attended, self_out_weight, preferred_element_type=jnp.float32)
        noise_pred = noise_pred + table[3] * jnp.dot(guided, cross_out_weight, preferred_element_type=jnp.float32)
        level_now = signal_level(moment)
        level_after = signal_level(after)
        current = state.astype(jnp.float32)
        clean = (current - jnp.sqrt(1.0 - level_now) * noise_pred) / jnp.sqrt(level_now)
        moved = jnp.sqrt(level_after) * clean + jnp.sqrt(1.0 - level_after) * noise_pred
        kept = jnp.sqrt(level_after) * known.astype(jnp.float32) + jnp.sqrt(1.0 - level_after) * latents.astype(jnp.float32)
        state = jnp.where(seam_mask[:, None] == 1, moved, kept).astype(jnp.bfloat16)
    return state
```

```python
import functools
import math

import jax
import jax.numpy as jnp
from jax import lax
from jax.experimental import pallas as pl
from jax.experimental.pallas import tpu as pltpu
from jax.sharding import PartitionSpec as P

D = 1024
HEAD_DIM = 64
FREQ = 256
BLOCK = 128
MAXK = 6
ROW = 4
STEPS = 2
LANES = 128
HALF = D // 2
F32 = jnp.float32
BF16 = jnp.bfloat16
VMEM_LIMIT = 30 * 1024 * 1024


def passed_along(block, axis, distance):
    devices = range(lax.axis_size(axis))
    route = [((i - distance) % len(devices), i) for i in devices]
    return lax.ppermute(block, axis, route)


def partner_swap(block, axis, mask):
    devices = range(lax.axis_size(axis))
    return lax.ppermute(block, axis, [(i ^ mask, i) for i in devices])


def signal_level(moment):
    angle = (moment.astype(F32) / 1000.0 + 0.008) / 1.008 * (math.pi / 2.0)
    cosine = jnp.cos(angle)
    return cosine * cosine


def modulation_tables(moments, modulation_weight):
    half = FREQ // 2
    frequency = jnp.exp(-math.log(10000.0) * jnp.arange(half, dtype=F32) / half)
    phase = moments.astype(F32)[:, None] * frequency[None, :]
    embed = jnp.concatenate([jnp.cos(phase), jnp.sin(phase)], axis=1)
    active = jax.nn.silu(embed).astype(BF16)
    width = modulation_weight.shape[2]
    table = jnp.dot(
        active, modulation_weight.reshape(FREQ, 4 * width), preferred_element_type=F32
    )
    return table.reshape(moments.shape[0], 4, width)


def call(body, out, ins, scratch=(), flops=0, moved=0):
    return pl.pallas_call(
        body,
        out_shape=out,
        in_specs=[pl.BlockSpec(memory_space=m) for m in ins],
        out_specs=jax.tree.map(lambda _: pl.BlockSpec(memory_space=pltpu.VMEM), out),
        scratch_shapes=list(scratch),
        compiler_params=pltpu.CompilerParams(vmem_limit_bytes=VMEM_LIMIT),
        cost_estimate=pl.CostEstimate(flops=flops, bytes_accessed=moved, transcendentals=0),
    )


def halves(h):
    near = pl.ds(pl.multiple_of(h * HALF, HALF), HALF)
    far = pl.ds(pl.multiple_of((1 - h) * HALF, HALF), HALF)
    return near, far


def normalize(near, far):
    near = near.astype(F32)
    far = far.astype(F32)
    width = near.shape[1] + far.shape[1]
    mean = (
        jnp.sum(near, axis=1, keepdims=True) + jnp.sum(far, axis=1, keepdims=True)
    ) / width
    near = near - mean
    far = far - mean
    second = (
        jnp.sum(near * near, axis=1, keepdims=True) + jnp.sum(far * far, axis=1, keepdims=True)
    ) / width
    gain = lax.rsqrt(second + 1e-06)
    return near * gain, far * gain


def modulate(normed, table_ref, side):
    return (normed * (1.0 + table_ref[1:2, side]) + table_ref[0:1, side]).astype(BF16)


def two_dots(a, b, weight_ref, near, far, lead=None):
    if lead is None:
        wa, wb = weight_ref[near, :], weight_ref[far, :]
    else:
        wa, wb = weight_ref[lead, near, :], weight_ref[lead, far, :]
    return jnp.dot(a, wa, preferred_element_type=F32) + jnp.dot(b, wb, preferred_element_type=F32)


def own_body(h_ref, near_ref, far_ref, table_ref, w_ref, cw_ref, q_ref, kv_ref, cq_ref):
    near, far = halves(h_ref[0])
    scale = 1.0 / math.sqrt(HEAD_DIM)
    na, nb = normalize(near_ref[...], far_ref[...])
    ma, mb = modulate(na, table_ref, near), modulate(nb, table_ref, far)
    kv_ref[:, :HALF] = two_dots(ma, mb, w_ref, near, far, 1).astype(BF16)
    kv_ref[:, HALF:] = two_dots(ma, mb, w_ref, near, far, 2).astype(BF16)
    q_ref[...] = (two_dots(ma, mb, w_ref, near, far, 0) * scale).astype(BF16)
    cq = two_dots(na.astype(BF16), nb.astype(BF16), cw_ref, near, far, 0)
    cq_ref[...] = (cq * scale).astype(BF16)


def away_body(h_ref, near_ref, far_ref, table_ref, w_ref, kv_ref):
    near, far = halves(h_ref[0])
    na, nb = normalize(near_ref[...], far_ref[...])
    ma, mb = modulate(na, table_ref, near), modulate(nb, table_ref, far)
    kv_ref[:, :HALF] = two_dots(ma, mb, w_ref, near, far, 1).astype(BF16)
    kv_ref[:, HALF:] = two_dots(ma, mb, w_ref, near, far, 2).astype(BF16)


def guide_body(rows_ref, cw_ref, kv_ref):
    rows = rows_ref[...].astype(F32)
    center = rows - jnp.mean(rows, axis=1, keepdims=True)
    second = jnp.mean(center * center, axis=1, keepdims=True)
    plain = (center * lax.rsqrt(second + 1e-06)).astype(BF16)
    kv_ref[:, :HALF] = jnp.dot(plain, cw_ref[1], preferred_element_type=F32).astype(BF16)
    kv_ref[:, HALF:] = jnp.dot(plain, cw_ref[2], preferred_element_type=F32).astype(BF16)


def pair_attention(query, keys, values, live):
    rows = query.shape[0]
    low = lax.broadcasted_iota(jnp.int32, (rows, LANES), 1) < HEAD_DIM
    zero = jnp.zeros_like(query)
    stacked = jnp.concatenate([jnp.where(low, query, zero), jnp.where(low, zero, query)], axis=0)
    scores = []
    for index, key in enumerate(keys):
        score = lax.dot_general(
            stacked, key, (((1,), (1,)), ((), ())), preferred_element_type=F32
        )
        if live is not None and live[index] is not None:
            score = jnp.where(live[index], score, -1e30)
        scores.append(score)
    peak = jnp.max(functools.reduce(jnp.maximum, scores), axis=1, keepdims=True)
    weights = [jnp.exp(score - peak) for score in scores]
    total = jnp.sum(functools.reduce(jnp.add, weights), axis=1, keepdims=True)
    mixed = None
    for weight, value in zip(weights, values):
        part = jnp.dot(weight.astype(BF16), value, preferred_element_type=F32)
        mixed = part if mixed is None else mixed + part
    mixed = mixed / total
    return jnp.where(low, mixed[:rows], mixed[rows:]).astype(BF16)


def cross_body(cq_ref, kv_ref, out_ref):
    rows = cq_ref.shape[0]
    count = kv_ref.shape[0]
    for block in range(rows // BLOCK):
        at = pl.ds(block * BLOCK, BLOCK)
        for pair in range(HALF // LANES):
            lane = pl.ds(pair * LANES, LANES)
            vlane = pl.ds(HALF + pair * LANES, LANES)
            keys = [kv_ref[pl.ds(g, BLOCK), lane] for g in range(0, count, BLOCK)]
            values = [kv_ref[pl.ds(g, BLOCK), vlane] for g in range(0, count, BLOCK)]
            out_ref[at, lane] = pair_attention(cq_ref[at, lane], keys, values, None)


def attend_body(
    h_ref, list_ref, q_ref, lower_ref, own_ref, upper_ref, row_lower_ref, row_upper_ref,
    guided_ref, table_ref, wo_ref, wc_ref, send_ref, keep_ref, window, attended,
):
    per_tile = q_ref.shape[0] // BLOCK
    tiles = (row_lower_ref, lower_ref, own_ref, upper_ref, row_upper_ref)
    for place, tile in enumerate(tiles):
        for block in range(per_tile):
            window[place * per_tile + block] = tile[pl.ds(block * BLOCK, BLOCK), :]
    for block in range(per_tile):
        at = pl.ds(block * BLOCK, BLOCK)
        entries = [list_ref[block, slot] for slot in range(MAXK)]
        live = [None] + [entry >= 0 for entry in entries[1:]]
        picked = [jnp.maximum(entry, 0) for entry in entries]
        for pair in range(HALF // LANES):
            lane = pl.ds(pair * LANES, LANES)
            vlane = pl.ds(HALF + pair * LANES, LANES)
            keys = [window[entry, :, lane] for entry in picked]
            values = [window[entry, :, vlane] for entry in picked]
            attended[at, lane] = pair_attention(q_ref[at, lane], keys, values, live)
    near, far = halves(h_ref[0])
    mine, guided = attended[...], guided_ref[...]
    for side, out_ref in ((far, send_ref), (near, keep_ref)):
        first = jnp.dot(mine, wo_ref[:, side], preferred_element_type=F32)
        second = jnp.dot(guided, wc_ref[:, side], preferred_element_type=F32)
        out_ref[...] = (table_ref[2:3, side] * first + table_ref[3:4, side] * second).astype(
            out_ref.dtype
        )


def on_device(
    latents,
    known,
    seam_mask,
    timesteps,
    block_lists,
    guidance,
    modulation_weight,
    self_weight,
    self_out_weight,
    cross_weight,
    cross_out_weight,
):
    cycle_size = lax.axis_size("seq")
    position = lax.axis_index("seq")
    side = lax.axis_index("head").astype(jnp.int32).reshape(1)
    tokens = latents.shape[0]
    per_tile = tokens // BLOCK
    vm, sm = pltpu.VMEM, pltpu.SMEM
    shape = jax.ShapeDtypeStruct

    source = block_lists // per_tile
    within = block_lists % per_tile
    offset = (source - position) % cycle_size
    place = jnp.where(
        offset == 0, 2, jnp.where(
            offset == 1, 3, jnp.where(
                offset == ROW % cycle_size, 4, jnp.where(offset == cycle_size - 1, 1, 0))))
    picked = jnp.where(block_lists >= 0, place * per_tile + within, -1).astype(jnp.int32)

    guide_count = guidance.shape[1]
    rows = guidance.reshape(1, STEPS * guide_count, D)
    mask = cycle_size // 2
    while mask:
        rows = jnp.concatenate([rows, partner_swap(rows, "seq", mask)], axis=0)
        mask //= 2
    rows = rows.reshape(-1, STEPS, guide_count, D)

    w_self = jnp.transpose(self_weight, (1, 0, 2))
    w_cross = jnp.transpose(cross_weight, (1, 0, 2))
    tables = modulation_tables(timesteps[:STEPS], modulation_weight)
    every = rows.shape[0] * guide_count

    state = latents
    for step in range(STEPS):
        table = tables[step]
        other = partner_swap(state, "head", 1)
        row_lower = passed_along(state, "seq", ROW)
        row_upper = passed_along(state, "seq", -ROW)
        query, pair, cross_query = call(
            own_body,
            (shape((tokens, HALF), BF16), shape((tokens, D), BF16), shape((tokens, HALF), BF16)),
            (sm, vm, vm, vm, vm, vm),
            flops=2 * tokens * D * 2 * D,
            moved=6 << 20,
        )(side, state, other, table, w_self, w_cross)
        lower = passed_along(pair, "seq", 1)
        upper = passed_along(pair, "seq", -1)
        row_pairs = []
        for half in (row_lower, row_upper):
            row_pairs.append(
                call(
                    away_body,
                    shape((tokens, D), BF16),
                    (sm, vm, vm, vm, vm),
                    flops=2 * tokens * D * D,
                    moved=4 << 20,
                )(side, half, partner_swap(half, "head", 1), table, w_self)
            )
        guide_pair = call(
            guide_body,
            shape((every, D), BF16),
            (vm, vm),
            flops=2 * every * D * D,
            moved=3 << 20,
        )(rows[:, step].reshape(every, D), w_cross)
        guided = call(
            cross_body,
            shape((tokens, HALF), BF16),
            (vm, vm),
            flops=8 * tokens * every * HALF,
            moved=1 << 20,
        )(cross_query, guide_pair)
        send, keep = call(
            attend_body,
            (shape((tokens, HALF), BF16), shape((tokens, HALF), F32)),
            (sm, sm) + (vm,) * 10,
            scratch=(vm((5 * per_tile, BLOCK, D), BF16), vm((tokens, HALF), BF16)),
            flops=8 * tokens * MAXK * BLOCK * HALF + 4 * tokens * HALF * D,
            moved=6 << 20,
        )(
            side, picked, query, lower, pair, upper, row_pairs[0], row_pairs[1],
            guided, table, self_out_weight, cross_out_weight,
        )
        noise_pred = keep + partner_swap(send, "head", 1).astype(F32)
        level_now = signal_level(timesteps[step])
        level_after = signal_level(timesteps[step + 1])
        current = state.astype(F32)
        clean = (current - jnp.sqrt(1.0 - level_now) * noise_pred) / jnp.sqrt(level_now)
        moved = jnp.sqrt(level_after) * clean + jnp.sqrt(1.0 - level_after) * noise_pred
        kept = jnp.sqrt(level_after) * known.astype(F32) + jnp.sqrt(
            1.0 - level_after
        ) * latents.astype(F32)
        state = jnp.where(seam_mask[:, None] == 1, moved, kept).astype(BF16)
    return state


def solution(mesh):
    in_specs = (
        P("seq", "head"),
        P("seq", "head"),
        P("seq"),
        P(),
        P("seq", None),
        P(None, "seq", None),
        P(),
        P(None, None, "head"),
        P("head", None),
        P(None, None, "head"),
        P("head", None),
    )
    out_specs = P("seq", "head")
    return jax.shard_map(
        on_device, mesh=mesh, in_specs=in_specs, out_specs=out_specs, check_vma=False
    )
```

```python
import functools
import math

import jax
import jax.numpy as jnp
from jax import lax
from jax.experimental import pallas as pl
from jax.experimental.pallas import tpu as pltpu
from jax.sharding import PartitionSpec as P

D = 1024
HEAD_DIM = 64
FREQ = 256
BLOCK = 128
MAXK = 6
ROW = 4
STEPS = 2
LANES = 128
HALF = D // 2
F32 = jnp.float32
BF16 = jnp.bfloat16
VMEM_LIMIT = 30 * 1024 * 1024


def passed_along(block, axis, distance):
    devices = range(lax.axis_size(axis))
    route = [((i - distance) % len(devices), i) for i in devices]
    return lax.ppermute(block, axis, route)


def partner_swap(block, axis, mask):
    devices = range(lax.axis_size(axis))
    return lax.ppermute(block, axis, [(i ^ mask, i) for i in devices])


def signal_level(moment):
    angle = (moment.astype(F32) / 1000.0 + 0.008) / 1.008 * (math.pi / 2.0)
    cosine = jnp.cos(angle)
    return cosine * cosine


def active_rows(moments):
    half = FREQ // 2
    frequency = jnp.exp(-math.log(10000.0) * jnp.arange(half, dtype=F32) / half)
    phase = moments.astype(F32)[:, None] * frequency[None, :]
    embed = jnp.concatenate([jnp.cos(phase), jnp.sin(phase)], axis=1)
    return jax.nn.silu(embed).astype(BF16)


def table_body(active_ref, weight_ref, *table_refs):
    for part in range(weight_ref.shape[0]):
        rows = jnp.dot(active_ref[...], weight_ref[part], preferred_element_type=F32)
        for step, table_ref in enumerate(table_refs):
            table_ref[part : part + 1, :] = rows[step : step + 1]


def call(body, out, ins, scratch=(), flops=0, moved=0):
    return pl.pallas_call(
        body,
        out_shape=out,
        in_specs=[pl.BlockSpec(memory_space=m) for m in ins],
        out_specs=jax.tree.map(lambda _: pl.BlockSpec(memory_space=pltpu.VMEM), out),
        scratch_shapes=list(scratch),
        compiler_params=pltpu.CompilerParams(vmem_limit_bytes=VMEM_LIMIT),
        cost_estimate=pl.CostEstimate(flops=flops, bytes_accessed=moved, transcendentals=0),
    )


def halves(h):
    near = pl.ds(pl.multiple_of(h * HALF, HALF), HALF)
    far = pl.ds(pl.multiple_of((1 - h) * HALF, HALF), HALF)
    return near, far


def normalize(near, far):
    near = near.astype(F32)
    far = far.astype(F32)
    width = near.shape[1] + far.shape[1]
    mean = (
        jnp.sum(near, axis=1, keepdims=True) + jnp.sum(far, axis=1, keepdims=True)
    ) / width
    near = near - mean
    far = far - mean
    second = (
        jnp.sum(near * near, axis=1, keepdims=True) + jnp.sum(far * far, axis=1, keepdims=True)
    ) / width
    gain = lax.rsqrt(second + 1e-06)
    return near * gain, far * gain


def modulate(normed, table_ref, side):
    return (normed * (1.0 + table_ref[1:2, side]) + table_ref[0:1, side]).astype(BF16)


def two_dots(a, b, weight_ref, near, far, lead=None):
    if lead is None:
        wa, wb = weight_ref[near, :], weight_ref[far, :]
    else:
        wa, wb = weight_ref[lead, near, :], weight_ref[lead, far, :]
    return jnp.dot(a, wa, preferred_element_type=F32) + jnp.dot(b, wb, preferred_element_type=F32)


def own_body(
    h_ref, near_ref, far_ref, table_ref, w_ref, cross_ref, q_ref, kv_ref, cq_ref, cw_ref, sem
):
    fetch = pltpu.make_async_copy(cross_ref.at[0], cw_ref, sem)
    fetch.start()
    near, far = halves(h_ref[0])
    scale = 1.0 / math.sqrt(HEAD_DIM)
    na, nb = normalize(near_ref[...], far_ref[...])
    ma, mb = modulate(na, table_ref, near), modulate(nb, table_ref, far)
    kv_ref[:, :HALF] = two_dots(ma, mb, w_ref, near, far, 1).astype(BF16)
    kv_ref[:, HALF:] = two_dots(ma, mb, w_ref, near, far, 2).astype(BF16)
    q_ref[...] = (two_dots(ma, mb, w_ref, near, far, 0) * scale).astype(BF16)
    fetch.wait()
    cq = two_dots(na.astype(BF16), nb.astype(BF16), cw_ref, near, far)
    cq_ref[...] = (cq * scale).astype(BF16)


def away_body(h_ref, near_ref, far_ref, table_ref, w_ref, kv_ref):
    near, far = halves(h_ref[0])
    na, nb = normalize(near_ref[...], far_ref[...])
    ma, mb = modulate(na, table_ref, near), modulate(nb, table_ref, far)
    kv_ref[:, :HALF] = two_dots(ma, mb, w_ref, near, far, 1).astype(BF16)
    kv_ref[:, HALF:] = two_dots(ma, mb, w_ref, near, far, 2).astype(BF16)


def guide_body(rows_ref, cw_ref, kv_ref):
    rows = rows_ref[...].astype(F32)
    center = rows - jnp.mean(rows, axis=1, keepdims=True)
    second = jnp.mean(center * center, axis=1, keepdims=True)
    plain = (center * lax.rsqrt(second + 1e-06)).astype(BF16)
    kv_ref[:, :HALF] = jnp.dot(plain, cw_ref[1], preferred_element_type=F32).astype(BF16)
    kv_ref[:, HALF:] = jnp.dot(plain, cw_ref[2], preferred_element_type=F32).astype(BF16)


def pair_attention(query, keys, values, live):
    rows = query.shape[0]
    low = lax.broadcasted_iota(jnp.int32, (rows, LANES), 1) < HEAD_DIM
    zero = jnp.zeros_like(query)
    stacked = jnp.concatenate([jnp.where(low, query, zero), jnp.where(low, zero, query)], axis=0)
    scores = []
    for index, key in enumerate(keys):
        score = lax.dot_general(
            stacked, key, (((1,), (1,)), ((), ())), preferred_element_type=F32
        )
        if live is not None and live[index] is not None:
            score = jnp.where(live[index], score, -1e30)
        scores.append(score)
    peak = jnp.max(functools.reduce(jnp.maximum, scores), axis=1, keepdims=True)
    weights = [jnp.exp(score - peak) for score in scores]
    total = jnp.sum(functools.reduce(jnp.add, weights), axis=1, keepdims=True)
    mixed = None
    for weight, value in zip(weights, values):
        part = jnp.dot(weight.astype(BF16), value, preferred_element_type=F32)
        mixed = part if mixed is None else mixed + part
    mixed = mixed / total
    return jnp.where(low, mixed[:rows], mixed[rows:]).astype(BF16)


def cross_body(cq_ref, kv_ref, out_ref):
    rows = cq_ref.shape[0]
    count = kv_ref.shape[0]
    for block in range(rows // BLOCK):
        at = pl.ds(block * BLOCK, BLOCK)
        for pair in range(HALF // LANES):
            lane = pl.ds(pair * LANES, LANES)
            vlane = pl.ds(HALF + pair * LANES, LANES)
            keys = [kv_ref[pl.ds(g, BLOCK), lane] for g in range(0, count, BLOCK)]
            values = [kv_ref[pl.ds(g, BLOCK), vlane] for g in range(0, count, BLOCK)]
            out_ref[at, lane] = pair_attention(cq_ref[at, lane], keys, values, None)


def attend_body(
    h_ref, list_ref, mix_ref, q_ref, lower_ref, own_ref, upper_ref, row_lower_ref, row_upper_ref,
    guided_ref, table_ref, wo_ref, wc_ref, state_ref, kept_ref, seam_ref,
    send_ref, base_ref, window, attended,
):
    per_tile = q_ref.shape[0] // BLOCK
    tiles = (row_lower_ref, lower_ref, own_ref, upper_ref, row_upper_ref)
    for place, tile in enumerate(tiles):
        for block in range(per_tile):
            window[place * per_tile + block] = tile[pl.ds(block * BLOCK, BLOCK), :]
    for block in range(per_tile):
        at = pl.ds(block * BLOCK, BLOCK)
        entries = [list_ref[block, slot] for slot in range(MAXK)]
        live = [None] + [entry >= 0 for entry in entries[1:]]
        picked = [jnp.maximum(entry, 0) for entry in entries]
        for pair in range(HALF // LANES):
            lane = pl.ds(pair * LANES, LANES)
            vlane = pl.ds(HALF + pair * LANES, LANES)
            keys = [window[entry, :, lane] for entry in picked]
            values = [window[entry, :, vlane] for entry in picked]
            attended[at, lane] = pair_attention(q_ref[at, lane], keys, values, live)
    near, far = halves(h_ref[0])
    mine, guided = attended[...], guided_ref[...]
    parts = []
    for side in (far, near):
        first = jnp.dot(mine, wo_ref[:, side], preferred_element_type=F32)
        second = jnp.dot(guided, wc_ref[:, side], preferred_element_type=F32)
        parts.append(table_ref[2:3, side] * first + table_ref[3:4, side] * second)
    send_ref[...] = parts[0].astype(BF16)
    moved = mix_ref[0] * state_ref[...].astype(F32) + mix_ref[1] * parts[1]
    base_ref[...] = jnp.where(seam_ref[...] == 1, moved, kept_ref[...])


def every_guide(guidance, cycle_size):
    steps, count, width = guidance.shape
    rows = guidance.reshape(1, steps * count, width)
    mask = cycle_size // 2
    while mask:
        rows = jnp.concatenate([rows, partner_swap(rows, "seq", mask)], axis=0)
        mask //= 2
    return rows.reshape(cycle_size, steps, count, width)


def on_device(
    latents,
    known,
    seam_mask,
    timesteps,
    block_lists,
    guidance,
    modulation_weight,
    self_weight,
    self_out_weight,
    cross_weight,
    cross_out_weight,
):
    cycle_size = lax.axis_size("seq")
    position = lax.axis_index("seq")
    side = lax.axis_index("head").astype(jnp.int32).reshape(1)
    tokens = latents.shape[0]
    per_tile = tokens // BLOCK
    vm, sm = pltpu.VMEM, pltpu.SMEM
    shape = jax.ShapeDtypeStruct

    source = block_lists // per_tile
    within = block_lists % per_tile
    offset = (source - position) % cycle_size
    place = jnp.where(
        offset == 0, 2, jnp.where(
            offset == 1, 3, jnp.where(
                offset == ROW % cycle_size, 4, jnp.where(offset == cycle_size - 1, 1, 0))))
    picked = jnp.where(block_lists >= 0, place * per_tile + within, -1).astype(jnp.int32)

    guide_count = guidance.shape[1]
    every = cycle_size * guide_count

    w_self = jnp.transpose(self_weight, (1, 0, 2))
    w_cross = jnp.transpose(cross_weight, (1, 0, 2))
    seam = seam_mask[:, None]
    level = signal_level(timesteps)
    root, rest = jnp.sqrt(level), jnp.sqrt(1.0 - level)
    active = jnp.pad(active_rows(timesteps[:STEPS]), ((0, 8 - STEPS), (0, 0)))
    tables = call(
        table_body,
        (shape((4, D), F32),) * STEPS,
        (vm, vm),
        flops=16 * FREQ * 4 * D,
        moved=2 << 20,
    )(active, jnp.transpose(modulation_weight, (1, 0, 2)))
    state = latents
    for step in range(STEPS):
        table = tables[step]
        other = partner_swap(state, "head", 1)
        row_lower = passed_along(state, "seq", ROW)
        row_upper = passed_along(state, "seq", -ROW)
        query, pair, cross_query = call(
            own_body,
            (shape((tokens, HALF), BF16), shape((tokens, D), BF16), shape((tokens, HALF), BF16)),
            (sm, vm, vm, vm, vm, pl.ANY),
            scratch=(vm((D, HALF), BF16), pltpu.SemaphoreType.DMA),
            flops=2 * tokens * D * 2 * D,
            moved=6 << 20,
        )(side, state, other, table, w_self, w_cross)
        if step == 0:
            rows, query = lax.optimization_barrier((guidance, query))
            rows = every_guide(rows, cycle_size)
        lower = passed_along(pair, "seq", 1)
        upper = passed_along(pair, "seq", -1)
        row_pairs = []
        for half in (row_lower, row_upper):
            row_pairs.append(
                call(
                    away_body,
                    shape((tokens, D), BF16),
                    (sm, vm, vm, vm, vm),
                    flops=2 * tokens * D * D,
                    moved=4 << 20,
                )(side, half, partner_swap(half, "head", 1), table, w_self)
            )
        guide_pair = call(
            guide_body,
            shape((every, D), BF16),
            (vm, vm),
            flops=2 * every * D * D,
            moved=3 << 20,
        )(rows[:, step].reshape(every, D), w_cross)
        guided = call(
            cross_body,
            shape((tokens, HALF), BF16),
            (vm, vm),
            flops=8 * tokens * every * HALF,
            moved=1 << 20,
        )(cross_query, guide_pair)
        kept = root[step + 1] * known.astype(F32) + rest[step + 1] * latents.astype(F32)
        ratio = root[step + 1] / root[step]
        mix = jnp.stack([ratio, rest[step + 1] - ratio * rest[step]])
        send, base = call(
            attend_body,
            (shape((tokens, HALF), BF16), shape((tokens, HALF), F32)),
            (sm, sm, sm) + (vm,) * 13,
            scratch=(vm((5 * per_tile, BLOCK, D), BF16), vm((tokens, HALF), BF16)),
            flops=8 * tokens * MAXK * BLOCK * HALF + 4 * tokens * HALF * D,
            moved=6 << 20,
        )(
            side, picked, mix, query, lower, pair, upper, row_pairs[0], row_pairs[1],
            guided, table, self_out_weight, cross_out_weight, state, kept, seam,
        )
        received = partner_swap(send, "head", 1).astype(F32)
        state = jnp.where(seam == 1, base + mix[1] * received, base).astype(BF16)
    return state


def solution(mesh):
    in_specs = (
        P("seq", "head"),
        P("seq", "head"),
        P("seq"),
        P(),
        P("seq", None),
        P(None, "seq", None),
        P(),
        P(None, None, "head"),
        P("head", None),
        P(None, None, "head"),
        P("head", None),
    )
    out_specs = P("seq", "head")
    return jax.shard_map(
        on_device, mesh=mesh, in_specs=in_specs, out_specs=out_specs, check_vma=False
    )
```

```python
import functools
import math

import jax
import jax.numpy as jnp
from jax import lax
from jax.experimental import pallas as pl
from jax.experimental.pallas import tpu as pltpu
from jax.sharding import PartitionSpec as P

D = 1024
HEAD_DIM = 64
FREQ = 256
BLOCK = 128
MAXK = 6
ROW = 4
STEPS = 2
LANES = 128
HALF = D // 2
F32 = jnp.float32
BF16 = jnp.bfloat16
VMEM_LIMIT = 16 * 1024 * 1024


def passed_along(block, axis, distance):
    devices = range(lax.axis_size(axis))
    route = [((i - distance) % len(devices), i) for i in devices]
    return lax.ppermute(block, axis, route)


def partner_swap(block, axis, mask):
    devices = range(lax.axis_size(axis))
    return lax.ppermute(block, axis, [(i ^ mask, i) for i in devices])


def table_body(times_ref, weight_ref, *table_refs):
    half = FREQ // 2
    row = lax.broadcasted_iota(jnp.int32, (8, LANES), 0)
    column = lax.broadcasted_iota(jnp.int32, (8, half), 1).astype(F32)
    moments = jnp.zeros((8, LANES), F32)
    for index in range(STEPS + 1):
        moments = jnp.where(row == index, times_ref[index].astype(F32), moments)
    phase = moments * jnp.exp(-math.log(10000.0) * column / half)
    cosine, sine = jnp.cos(phase), jnp.sin(phase)
    cosine = (cosine * jax.nn.sigmoid(cosine)).astype(BF16)
    sine = (sine * jax.nn.sigmoid(sine)).astype(BF16)
    for part in range(weight_ref.shape[0]):
        rows = jnp.dot(cosine, weight_ref[part, :half, :], preferred_element_type=F32)
        rows = rows + jnp.dot(sine, weight_ref[part, half:, :], preferred_element_type=F32)
        for step, table_ref in enumerate(table_refs):
            table_ref[part : part + 1, :] = rows[step : step + 1]
    level = jnp.cos((moments / 1000.0 + 0.008) / 1.008 * (math.pi / 2.0))
    level = level * level
    root, rest = jnp.sqrt(level), jnp.sqrt(1.0 - level)
    for step, table_ref in enumerate(table_refs):
        root_after, rest_after = root[step + 1 : step + 2, :1], rest[step + 1 : step + 2, :1]
        ratio = root_after / root[step : step + 1, :1]
        gain = rest_after - ratio * rest[step : step + 1, :1]
        for place, value in enumerate((ratio, gain, root_after, rest_after)):
            table_ref[4 + place : 5 + place, :] = jnp.broadcast_to(value, (1, D))


def call(body, out, ins, scratch=(), flops=0, moved=0):
    return pl.pallas_call(
        body,
        out_shape=out,
        in_specs=[pl.BlockSpec(memory_space=m) for m in ins],
        out_specs=jax.tree.map(lambda _: pl.BlockSpec(memory_space=pltpu.VMEM), out),
        scratch_shapes=list(scratch),
        compiler_params=pltpu.CompilerParams(vmem_limit_bytes=VMEM_LIMIT),
        cost_estimate=pl.CostEstimate(flops=flops, bytes_accessed=moved, transcendentals=0),
    )


def halves():
    h = lax.axis_index("head")
    near = pl.ds(pl.multiple_of(h * HALF, HALF), HALF)
    far = pl.ds(pl.multiple_of((1 - h) * HALF, HALF), HALF)
    return near, far


def normalize(near, far):
    near = near.astype(F32)
    far = far.astype(F32)
    width = near.shape[1] + far.shape[1]
    mean = (
        jnp.sum(near, axis=1, keepdims=True) + jnp.sum(far, axis=1, keepdims=True)
    ) / width
    near = near - mean
    far = far - mean
    second = (
        jnp.sum(near * near, axis=1, keepdims=True) + jnp.sum(far * far, axis=1, keepdims=True)
    ) / width
    gain = lax.rsqrt(second + 1e-06)
    return near * gain, far * gain


def modulate(normed, table_ref, side):
    return (normed * (1.0 + table_ref[1:2, side]) + table_ref[0:1, side]).astype(BF16)


def two_dots(a, b, weight_ref, near, far, lead=None):
    if lead is None:
        wa, wb = weight_ref[near, :], weight_ref[far, :]
    else:
        wa, wb = weight_ref[lead, near, :], weight_ref[lead, far, :]
    return jnp.dot(a, wa, preferred_element_type=F32) + jnp.dot(b, wb, preferred_element_type=F32)


def own_body(
    near_ref, far_ref, table_ref, w_ref, cross_ref, q_ref, kv_ref, cq_ref, cw_ref, sem
):
    fetch = pltpu.make_async_copy(cross_ref.at[0], cw_ref, sem)
    fetch.start()
    near, far = halves()
    scale = 1.0 / math.sqrt(HEAD_DIM)
    na, nb = normalize(near_ref[...], far_ref[...])
    ma, mb = modulate(na, table_ref, near), modulate(nb, table_ref, far)
    kv_ref[:, :HALF] = two_dots(ma, mb, w_ref, near, far, 1).astype(BF16)
    kv_ref[:, HALF:] = two_dots(ma, mb, w_ref, near, far, 2).astype(BF16)
    q_ref[...] = (two_dots(ma, mb, w_ref, near, far, 0) * scale).astype(BF16)
    fetch.wait()
    cq = two_dots(na.astype(BF16), nb.astype(BF16), cw_ref, near, far)
    cq_ref[...] = (cq * scale).astype(BF16)


def away_body(near_ref, far_ref, table_ref, w_ref, kv_ref):
    near, far = halves()
    na, nb = normalize(near_ref[...], far_ref[...])
    ma, mb = modulate(na, table_ref, near), modulate(nb, table_ref, far)
    kv_ref[:, :HALF] = two_dots(ma, mb, w_ref, near, far, 1).astype(BF16)
    kv_ref[:, HALF:] = two_dots(ma, mb, w_ref, near, far, 2).astype(BF16)


def guide_body(rows_ref, cw_ref, *kv_refs):
    rows = rows_ref[...].astype(F32)
    center = rows - jnp.mean(rows, axis=1, keepdims=True)
    second = jnp.mean(center * center, axis=1, keepdims=True)
    plain = (center * lax.rsqrt(second + 1e-06)).astype(BF16)
    count = kv_refs[0].shape[0]
    for part in range(2):
        both = jnp.dot(plain, cw_ref[part + 1], preferred_element_type=F32)
        both = both.reshape(-1, STEPS, 8, HALF)
        for step, kv_ref in enumerate(kv_refs):
            kv_ref[:, part * HALF : (part + 1) * HALF] = (
                both[:, step].reshape(count, HALF).astype(BF16)
            )


def pair_attention(query, keys, values, live):
    rows = query.shape[0]
    low = lax.broadcasted_iota(jnp.int32, (rows, LANES), 1) < HEAD_DIM
    zero = jnp.zeros_like(query)
    stacked = jnp.concatenate([jnp.where(low, query, zero), jnp.where(low, zero, query)], axis=0)
    scores = []
    for index, key in enumerate(keys):
        score = lax.dot_general(
            stacked, key, (((1,), (1,)), ((), ())), preferred_element_type=F32
        )
        if live is not None and live[index] is not None:
            score = jnp.where(live[index], score, -1e30)
        scores.append(score)
    peak = jnp.max(functools.reduce(jnp.maximum, scores), axis=1, keepdims=True)
    weights = [jnp.exp(score - peak) for score in scores]
    total = jnp.sum(functools.reduce(jnp.add, weights), axis=1, keepdims=True)
    mixed = None
    for weight, value in zip(weights, values):
        part = jnp.dot(weight.astype(BF16), value, preferred_element_type=F32)
        mixed = part if mixed is None else mixed + part
    mixed = mixed / total
    return jnp.where(low, mixed[:rows], mixed[rows:]).astype(BF16)


def cross_body(cq_ref, kv_ref, out_ref):
    rows = cq_ref.shape[0]
    count = kv_ref.shape[0]
    for block in range(rows // BLOCK):
        at = pl.ds(block * BLOCK, BLOCK)
        for pair in range(HALF // LANES):
            lane = pl.ds(pair * LANES, LANES)
            vlane = pl.ds(HALF + pair * LANES, LANES)
            keys = [kv_ref[pl.ds(g, BLOCK), lane] for g in range(0, count, BLOCK)]
            values = [kv_ref[pl.ds(g, BLOCK), vlane] for g in range(0, count, BLOCK)]
            out_ref[at, lane] = pair_attention(cq_ref[at, lane], keys, values, None)


def seam_column(seam_ref, block):
    shape = (BLOCK, BLOCK)
    same = lax.broadcasted_iota(jnp.int32, shape, 0) == lax.broadcasted_iota(jnp.int32, shape, 1)
    spread = jnp.broadcast_to(seam_ref[block : block + 1, :].astype(F32), shape)
    return jnp.sum(jnp.where(same, spread, 0.0), axis=1, keepdims=True) > 0.5


def attend_body(
    list_ref, q_ref, lower_ref, own_ref, upper_ref, row_lower_ref, row_upper_ref,
    guided_ref, table_ref, wo_ref, wc_ref, state_ref, known_ref, latent_ref, seam_ref,
    send_ref, base_ref, window, attended,
):
    per_tile = q_ref.shape[0] // BLOCK
    cycle = lax.axis_size("seq")
    position = lax.axis_index("seq")
    tiles = (row_lower_ref, lower_ref, own_ref, upper_ref, row_upper_ref)
    for place, tile in enumerate(tiles):
        for block in range(per_tile):
            window[place * per_tile + block] = tile[pl.ds(block * BLOCK, BLOCK), :]
    for block in range(per_tile):
        at = pl.ds(block * BLOCK, BLOCK)
        live, picked = [], []
        for slot in range(MAXK):
            entry = list_ref[block, slot]
            valid = entry >= 0
            tile = lax.div(jnp.maximum(entry, 0), per_tile)
            offset = tile - position
            offset = jnp.where(offset < 0, offset + cycle, offset)
            place = jnp.where(offset == ROW % cycle, 4, 0)
            place = jnp.where(offset == cycle - 1, 1, place)
            place = jnp.where(offset == 1, 3, place)
            place = jnp.where(jnp.logical_or(offset == 0, entry < 0), 2, place)
            live.append(None if slot == 0 else valid)
            picked.append(place * per_tile + lax.rem(jnp.maximum(entry, 0), per_tile))
        for pair in range(HALF // LANES):
            lane = pl.ds(pair * LANES, LANES)
            vlane = pl.ds(HALF + pair * LANES, LANES)
            keys = [window[entry, :, lane] for entry in picked]
            values = [window[entry, :, vlane] for entry in picked]
            attended[at, lane] = pair_attention(q_ref[at, lane], keys, values, live)
    near, far = halves()
    mine, guided = attended[...], guided_ref[...]
    parts = []
    for side in (far, near):
        first = jnp.dot(mine, wo_ref[:, side], preferred_element_type=F32)
        second = jnp.dot(guided, wc_ref[:, side], preferred_element_type=F32)
        parts.append(table_ref[2:3, side] * first + table_ref[3:4, side] * second)
    send_ref[...] = parts[0].astype(BF16)
    ratio, gain = table_ref[4:5, :HALF], table_ref[5:6, :HALF]
    root_after, rest_after = table_ref[6:7, :HALF], table_ref[7:8, :HALF]
    moved = ratio * state_ref[...].astype(F32) + gain * parts[1]
    kept = root_after * known_ref[...].astype(F32) + rest_after * latent_ref[...].astype(F32)
    for block in range(per_tile):
        rows = slice(block * BLOCK, (block + 1) * BLOCK)
        base_ref[rows, :] = jnp.where(seam_column(seam_ref, block), moved[rows], kept[rows])


def finish_body(base_ref, received_ref, seam_ref, table_ref, state_ref):
    gain = table_ref[5:6, :HALF]
    for block in range(base_ref.shape[0] // BLOCK):
        rows = slice(block * BLOCK, (block + 1) * BLOCK)
        base = base_ref[rows, :]
        moved = base + gain * received_ref[rows, :].astype(F32)
        state_ref[rows, :] = jnp.where(seam_column(seam_ref, block), moved, base).astype(BF16)


def every_guide(guidance, cycle_size):
    steps, count, width = guidance.shape
    rows = guidance.reshape(steps * count, width)
    mask = cycle_size // 2
    while mask:
        rows = jnp.concatenate([rows, partner_swap(rows, "seq", mask)], axis=0)
        mask //= 2
    return rows


def on_device(
    latents,
    known,
    seam_mask,
    timesteps,
    block_lists,
    guidance,
    modulation_weight,
    self_weight,
    self_out_weight,
    cross_weight,
    cross_out_weight,
):
    cycle_size = lax.axis_size("seq")
    tokens = latents.shape[0]
    vm, sm = pltpu.VMEM, pltpu.SMEM
    shape = jax.ShapeDtypeStruct
    every = cycle_size * guidance.shape[1]

    w_self = jnp.transpose(self_weight, (1, 0, 2))
    w_cross = jnp.transpose(cross_weight, (1, 0, 2))
    seam = seam_mask.reshape(tokens // BLOCK, BLOCK)
    tables = call(
        table_body,
        (shape((8, D), F32),) * STEPS,
        (sm, vm),
        flops=16 * FREQ * 4 * D,
        moved=2 << 20,
    )(timesteps, jnp.transpose(modulation_weight, (1, 0, 2)))

    state = latents
    for step in range(STEPS):
        table = tables[step]
        other = partner_swap(state, "head", 1)
        row_lower = passed_along(state, "seq", ROW)
        row_upper = passed_along(state, "seq", -ROW)
        query, pair, cross_query = call(
            own_body,
            (shape((tokens, HALF), BF16), shape((tokens, D), BF16), shape((tokens, HALF), BF16)),
            (vm, vm, vm, vm, pl.ANY),
            scratch=(vm((D, HALF), BF16), pltpu.SemaphoreType.DMA),
            flops=2 * tokens * D * 2 * D,
            moved=6 << 20,
        )(state, other, table, w_self, w_cross)
        lower = passed_along(pair, "seq", 1)
        upper = passed_along(pair, "seq", -1)
        if step == 0:
            rows, query = lax.optimization_barrier((guidance, query))
            guide_pairs = call(
                guide_body,
                (shape((every, D), BF16),) * STEPS,
                (vm, vm),
                flops=2 * STEPS * every * D * D,
                moved=3 << 20,
            )(every_guide(rows, cycle_size), w_cross)
        row_pairs = []
        for half in (row_lower, row_upper):
            row_pairs.append(
                call(
                    away_body,
                    shape((tokens, D), BF16),
                    (vm, vm, vm, vm),
                    flops=2 * tokens * D * D,
                    moved=4 << 20,
                )(half, partner_swap(half, "head", 1), table, w_self)
            )
        guided = call(
            cross_body,
            shape((tokens, HALF), BF16),
            (vm, vm),
            flops=8 * tokens * every * HALF,
            moved=1 << 20,
        )(cross_query, guide_pairs[step])
        send, base = call(
            attend_body,
            (shape((tokens, HALF), BF16), shape((tokens, HALF), F32)),
            (sm,) + (vm,) * 14,
            scratch=(
                vm((5 * tokens // BLOCK, BLOCK, D), BF16),
                vm((tokens, HALF), BF16),
            ),
            flops=8 * tokens * MAXK * BLOCK * HALF + 4 * tokens * HALF * D,
            moved=6 << 20,
        )(
            block_lists, query, lower, pair, upper, row_pairs[0], row_pairs[1],
            guided, table, self_out_weight, cross_out_weight, state, known, latents, seam,
        )
        state = call(
            finish_body,
            shape((tokens, HALF), BF16),
            (vm, vm, vm, vm),
            flops=4 * tokens * HALF,
            moved=1 << 20,
        )(base, partner_swap(send, "head", 1), seam, table)
    return state


def solution(mesh):
    in_specs = (
        P("seq", "head"),
        P("seq", "head"),
        P("seq"),
        P(),
        P("seq", None),
        P(None, "seq", None),
        P(),
        P(None, None, "head"),
        P("head", None),
        P(None, None, "head"),
        P("head", None),
    )
    out_specs = P("seq", "head")
    return jax.shard_map(
        on_device, mesh=mesh, in_specs=in_specs, out_specs=out_specs, check_vma=False
    )
```

```python
import functools
import math

import jax
import jax.numpy as jnp
from jax import lax
from jax.experimental import pallas as pl
from jax.experimental.pallas import tpu as pltpu
from jax.sharding import PartitionSpec as P


D = 1024
HEAD_DIM = 64
FREQ = 256
BLOCK = 128
MAXK = 6
ROW = 4
STEPS = 2
LANES = 128
HALF = D // 2
F32 = jnp.float32
BF16 = jnp.bfloat16
VMEM_LIMIT = 16 * 1024 * 1024


def pairing(size, stride, first):
    route = []
    for i in range(size):
        even = (i // stride) % 2 == 0
        route.append((i, (i + (stride if even == first else -stride)) % size))
    return route


def exchanged(block, axis, stride, first):
    return lax.ppermute(block, axis, pairing(lax.axis_size(axis), stride, first))


def partner_swap(block, axis, mask):
    return lax.ppermute(block, axis, [(i ^ mask, i) for i in range(lax.axis_size(axis))])


def table_body(times_ref, weight_ref, latent_hbm, known_hbm, *refs):
    table_refs = refs[:STEPS]
    latent_ref, known_ref, latent_sem, known_sem = refs[STEPS:]
    latent_copy = pltpu.make_async_copy(latent_hbm, latent_ref, latent_sem)
    known_copy = pltpu.make_async_copy(known_hbm, known_ref, known_sem)
    latent_copy.start()
    known_copy.start()
    half = FREQ // 2
    row = lax.broadcasted_iota(jnp.int32, (8, LANES), 0)
    column = lax.broadcasted_iota(jnp.int32, (8, half), 1).astype(F32)
    moments = jnp.zeros((8, LANES), F32)
    for index in range(STEPS + 1):
        moments = jnp.where(row == index, times_ref[index].astype(F32), moments)
    phase = moments * jnp.exp(-math.log(10000.0) * column / half)
    cosine, sine = jnp.cos(phase), jnp.sin(phase)
    cosine = (cosine * jax.nn.sigmoid(cosine)).astype(BF16)
    sine = (sine * jax.nn.sigmoid(sine)).astype(BF16)
    for part in range(weight_ref.shape[0]):
        rows = jnp.dot(cosine, weight_ref[part, :half, :], preferred_element_type=F32)
        rows = rows + jnp.dot(sine, weight_ref[part, half:, :], preferred_element_type=F32)
        for step, table_ref in enumerate(table_refs):
            table_ref[part : part + 1, :] = rows[step : step + 1]
    level = jnp.cos((moments / 1000.0 + 0.008) / 1.008 * (math.pi / 2.0))
    level = level * level
    root, rest = jnp.sqrt(level), jnp.sqrt(1.0 - level)
    for step, table_ref in enumerate(table_refs):
        root_after, rest_after = root[step + 1 : step + 2, :1], rest[step + 1 : step + 2, :1]
        ratio = root_after / root[step : step + 1, :1]
        gain = rest_after - ratio * rest[step : step + 1, :1]
        for place, value in enumerate((ratio, gain, root_after, rest_after)):
            table_ref[4 + place : 5 + place, :] = jnp.broadcast_to(value, (1, D))
    latent_copy.wait()
    known_copy.wait()


def call(body, out, ins, scratch=(), flops=0, moved=0):
    return pl.pallas_call(
        body,
        out_shape=out,
        in_specs=[pl.BlockSpec(memory_space=m) for m in ins],
        out_specs=jax.tree.map(lambda _: pl.BlockSpec(memory_space=pltpu.VMEM), out),
        scratch_shapes=list(scratch),
        compiler_params=pltpu.CompilerParams(vmem_limit_bytes=VMEM_LIMIT),
        cost_estimate=pl.CostEstimate(flops=flops, bytes_accessed=moved, transcendentals=0),
    )


def halves():
    h = lax.axis_index("head")
    near = pl.ds(pl.multiple_of(h * HALF, HALF), HALF)
    far = pl.ds(pl.multiple_of((1 - h) * HALF, HALF), HALF)
    return near, far


def normalize(near, far):
    near = near.astype(F32)
    far = far.astype(F32)
    width = near.shape[1] + far.shape[1]
    mean = (
        jnp.sum(near, axis=1, keepdims=True) + jnp.sum(far, axis=1, keepdims=True)
    ) / width
    near = near - mean
    far = far - mean
    second = (
        jnp.sum(near * near, axis=1, keepdims=True) + jnp.sum(far * far, axis=1, keepdims=True)
    ) / width
    gain = lax.rsqrt(second + 1e-06)
    return near * gain, far * gain


def modulate(normed, table_ref, side):
    return (normed * (1.0 + table_ref[1:2, side]) + table_ref[0:1, side]).astype(BF16)


def two_dots(a, b, weight_ref, near, far, lead=None):
    if lead is None:
        wa, wb = weight_ref[near, :], weight_ref[far, :]
    else:
        wa, wb = weight_ref[lead, near, :], weight_ref[lead, far, :]
    return jnp.dot(a, wa, preferred_element_type=F32) + jnp.dot(b, wb, preferred_element_type=F32)


def own_body(near_ref, far_ref, table_ref, w_ref, kv_ref, tail_ref, mixed_ref, plain_ref):
    near, far = halves()
    na, nb = normalize(near_ref[...], far_ref[...])
    ma, mb = modulate(na, table_ref, near), modulate(nb, table_ref, far)
    kv_ref[:, :HALF] = two_dots(ma, mb, w_ref, near, far, 1).astype(BF16)
    kv_ref[:, HALF:] = two_dots(ma, mb, w_ref, near, far, 2).astype(BF16)
    tail_ref[...] = kv_ref[kv_ref.shape[0] - tail_ref.shape[0] :, :]
    mixed_ref[:, :HALF], mixed_ref[:, HALF:] = ma, mb
    plain_ref[:, :HALF], plain_ref[:, HALF:] = na.astype(BF16), nb.astype(BF16)


def query_body(mixed_ref, plain_ref, w_ref, cross_ref, q_ref, cq_ref, cw_ref, sem):
    fetch = pltpu.make_async_copy(cross_ref.at[0], cw_ref, sem)
    fetch.start()
    near, far = halves()
    scale = math.log2(math.e) / math.sqrt(HEAD_DIM)
    query = two_dots(mixed_ref[:, :HALF], mixed_ref[:, HALF:], w_ref, near, far, 0)
    q_ref[...] = (query * scale).astype(BF16)
    fetch.wait()
    query = two_dots(plain_ref[:, :HALF], plain_ref[:, HALF:], cw_ref, near, far)
    cq_ref[...] = (query * scale).astype(BF16)


def away_body(near_ref, far_ref, table_ref, w_ref, kv_ref):
    near, far = halves()
    na, nb = normalize(near_ref[...], far_ref[...])
    ma, mb = modulate(na, table_ref, near), modulate(nb, table_ref, far)
    kv_ref[:, :HALF] = two_dots(ma, mb, w_ref, near, far, 1).astype(BF16)
    kv_ref[:, HALF:] = two_dots(ma, mb, w_ref, near, far, 2).astype(BF16)


def guide_body(step, each, rows_ref, cw_ref, kv_ref):
    rows = rows_ref[...].astype(F32).reshape(-1, STEPS, each, D)[:, step].reshape(-1, D)
    center = rows - jnp.mean(rows, axis=1, keepdims=True)
    second = jnp.mean(center * center, axis=1, keepdims=True)
    plain = (center * lax.rsqrt(second + 1e-06)).astype(BF16)
    for part in range(2):
        both = jnp.dot(plain, cw_ref[part + 1], preferred_element_type=F32)
        kv_ref[:, part * HALF : (part + 1) * HALF] = both.astype(BF16)


def join_body(kept_ref, received_ref, out_ref):
    count = kept_ref.shape[0]
    out_ref[:count, :] = kept_ref[...]
    out_ref[count:, :] = received_ref[...]


def pair_scores(query, keys, live, held):
    rows = query.shape[0]
    low = lax.broadcasted_iota(jnp.int32, (rows, LANES), 1) < HEAD_DIM
    zero = jnp.zeros_like(query)
    stacked = jnp.concatenate([jnp.where(low, query, zero), jnp.where(low, zero, query)], axis=0)
    peak = None
    for index, key in enumerate(keys):
        score = lax.dot_general(
            stacked, key, (((1,), (1,)), ((), ())), preferred_element_type=F32
        )
        if live is not None and live[index] is not None:
            score = jnp.where(live[index], score, -1e30)
        held[index] = score
        peak = score if peak is None else jnp.maximum(peak, score)
    return jnp.max(peak, axis=1, keepdims=True)


def pair_mixed(peak, values, held):
    rows = held.shape[1] // 2
    low = lax.broadcasted_iota(jnp.int32, (rows, LANES), 1) < HEAD_DIM
    total, mixed = None, None
    for index, value in enumerate(values):
        weight = jnp.exp2(held[index] - peak)
        part = jnp.dot(weight.astype(BF16), value, preferred_element_type=F32)
        total = weight if total is None else total + weight
        mixed = part if mixed is None else mixed + part
    total = jnp.sum(total, axis=1, keepdims=True)
    chosen = jnp.where(low, mixed[:rows], mixed[rows:])
    return (chosen / jnp.where(low, total[:rows], total[rows:])).astype(BF16)


def attention(count, query_of, keys_of, values_of, live, held, store):
    peaks = [pair_scores(query_of(0), keys_of(0), live, held.at[0])]
    for pair in range(count):
        if pair + 1 < count:
            ahead = held.at[(pair + 1) % 2]
            peaks.append(pair_scores(query_of(pair + 1), keys_of(pair + 1), live, ahead))
        store(pair, pair_mixed(peaks[pair], values_of(pair), held.at[pair % 2]))


def cross_body(cq_ref, kv_ref, out_ref, held):
    count = kv_ref.shape[0]
    for block in range(cq_ref.shape[0] // BLOCK):
        at = pl.ds(block * BLOCK, BLOCK)

        def store(pair, value):
            out_ref[at, pl.ds(pair * LANES, LANES)] = value

        def columns(start):
            lanes = pl.ds(start, LANES)
            return [kv_ref[pl.ds(g, BLOCK), lanes] for g in range(0, count, BLOCK)]

        attention(
            HALF // LANES,
            lambda pair: cq_ref[at, pl.ds(pair * LANES, LANES)],
            lambda pair: columns(pair * LANES),
            lambda pair: columns(HALF + pair * LANES),
            None,
            held,
            store,
        )


def seam_column(seam_ref, block):
    shape = (BLOCK, BLOCK)
    same = lax.broadcasted_iota(jnp.int32, shape, 0) == lax.broadcasted_iota(jnp.int32, shape, 1)
    spread = jnp.broadcast_to(seam_ref[block : block + 1, :].astype(F32), shape)
    return jnp.sum(jnp.where(same, spread, 0.0), axis=1, keepdims=True) > 0.5


def first_block_body(
    list_ref, q_ref, own_ref, side_a_ref, side_b_ref, head_a_ref, tail_a_ref, row_b_ref,
    guided_ref, table_ref, wo_ref, wc_ref, send_ref, attended_ref, window, held,
):
    filled = 0
    for tile in (own_ref, side_a_ref, side_b_ref, head_a_ref, tail_a_ref, row_b_ref):
        for block in range(tile.shape[0] // BLOCK):
            window[filled] = tile[pl.ds(block * BLOCK, BLOCK), :]
            filled += 1
    later_block_body(
        0, list_ref, q_ref, window, guided_ref, table_ref, wo_ref, wc_ref, send_ref, attended_ref,
        held,
    )


def projected(attended_ref, guided, table_ref, wo_ref, wc_ref, side):
    first = jnp.dot(attended_ref[...], wo_ref[:, side], preferred_element_type=F32)
    second = jnp.dot(guided, wc_ref[:, side], preferred_element_type=F32)
    return table_ref[2:3, side] * first + table_ref[3:4, side] * second


def later_block_body(
    block, list_ref, q_ref, window, guided_ref, table_ref, wo_ref, wc_ref, send_ref, attended_ref,
    held,
):
    per_tile = q_ref.shape[0] // BLOCK
    cycle = lax.axis_size("seq")
    position = lax.axis_index("seq")
    side_up = 1 + lax.rem(position, 2)
    row_up = 3 + lax.rem(lax.div(position, ROW), 2)
    at = pl.ds(block * BLOCK, BLOCK)
    live, picked = [], []
    for slot in range(MAXK):
        entry = list_ref[block, slot]
        tile = lax.div(jnp.maximum(entry, 0), per_tile)
        offset = tile - position
        offset = jnp.where(offset < 0, offset + cycle, offset)
        place = jnp.where(offset == ROW % cycle, row_up, 7 - row_up)
        place = jnp.where(offset == cycle - 1, 3 - side_up, place)
        place = jnp.where(offset == 1, side_up, place)
        place = jnp.where(jnp.logical_or(offset == 0, entry < 0), 0, place)
        live.append(None if slot == 0 else entry >= 0)
        picked.append(place * per_tile + lax.rem(jnp.maximum(entry, 0), per_tile))

    def store(pair, value):
        attended_ref[:, pl.ds(pair * LANES, LANES)] = value

    def columns(start):
        return [window[entry, :, pl.ds(start, LANES)] for entry in picked]

    attention(
        HALF // LANES,
        lambda pair: q_ref[at, pl.ds(pair * LANES, LANES)],
        lambda pair: columns(pair * LANES),
        lambda pair: columns(HALF + pair * LANES),
        live,
        held,
        store,
    )
    _, far = halves()
    part = projected(attended_ref, guided_ref[at, :], table_ref, wo_ref, wc_ref, far)
    send_ref[...] = part.astype(BF16)


def base_body(
    guided_ref, table_ref, wo_ref, wc_ref, state_ref, known_ref, latent_ref, seam_ref, *refs
):
    near, _ = halves()
    ratio, gain = table_ref[4:5, :HALF], table_ref[5:6, :HALF]
    root_after, rest_after = table_ref[6:7, :HALF], table_ref[7:8, :HALF]
    base_ref = refs[-1]
    for block, attended_ref in enumerate(refs[:-1]):
        rows = slice(block * BLOCK, (block + 1) * BLOCK)
        kept_part = projected(attended_ref, guided_ref[rows, :], table_ref, wo_ref, wc_ref, near)
        moved = ratio * state_ref[rows, :].astype(F32) + gain * kept_part
        kept = root_after * known_ref[rows, :].astype(F32)
        kept = kept + rest_after * latent_ref[rows, :].astype(F32)
        base_ref[rows, :] = jnp.where(seam_column(seam_ref, block), moved, kept)


def finish_body(blocks, base_ref, seam_ref, table_ref, *refs):
    gain = table_ref[5:6, :HALF]
    state_ref = refs[blocks]
    for block, received_ref in enumerate(refs[:blocks]):
        rows = slice(block * BLOCK, (block + 1) * BLOCK)
        base = base_ref[rows, :]
        moved = base + gain * received_ref[...].astype(F32)
        state_ref[rows, :] = jnp.where(seam_column(seam_ref, block), moved, base).astype(BF16)
    for head_ref in refs[blocks + 1 :]:
        head_ref[...] = state_ref[: head_ref.shape[0], :]


def every_guide(guidance, cycle_size):
    steps, count, width = guidance.shape
    rows = guidance.reshape(steps * count, width)
    bits = cycle_size.bit_length() - 1
    for bit in (*range(2, bits), 1, 0):
        received = partner_swap(rows, "seq", 1 << bit)
        rows = call(
            join_body,
            jax.ShapeDtypeStruct((2 * rows.shape[0], width), BF16),
            (pltpu.VMEM, pltpu.VMEM),
            moved=rows.size * 4,
        )(rows, received)
    return rows


def on_device(
    latents,
    known,
    seam_mask,
    timesteps,
    block_lists,
    guidance,
    modulation_weight,
    self_weight,
    self_out_weight,
    cross_weight,
    cross_out_weight,
):
    cycle_size = lax.axis_size("seq")
    tokens = latents.shape[0]
    vm, sm = pltpu.VMEM, pltpu.SMEM
    shape = jax.ShapeDtypeStruct
    every = cycle_size * guidance.shape[1]

    w_self = jnp.transpose(self_weight, (1, 0, 2))
    w_cross = jnp.transpose(cross_weight, (1, 0, 2))
    seam = seam_mask.reshape(tokens // BLOCK, BLOCK)
    state, head = latents, latents[: tokens // 2]
    for step in range(STEPS):
        other = partner_swap(state, "head", 1)
        row_b = exchanged(state, "seq", ROW, False)
        row_a = exchanged(head, "seq", ROW, True)
        if step == 0:
            *tables, latents, known = call(
                table_body,
                (shape((8, D), F32),) * STEPS + (shape((tokens, HALF), BF16),) * 2,
                (sm, vm, pl.ANY, pl.ANY),
                scratch=(pltpu.SemaphoreType.DMA,) * 2,
                flops=16 * FREQ * 4 * D,
                moved=2 << 20,
            )(timesteps, jnp.transpose(modulation_weight, (1, 0, 2)), latents, known)
            state = latents
        table = tables[step]
        pair, tail, mixed, plain = call(
            own_body,
            (
                shape((tokens, D), BF16),
                shape((tokens // 2, D), BF16),
                shape((tokens, D), BF16),
                shape((tokens, D), BF16),
            ),
            (vm, vm, vm, vm),
            flops=2 * tokens * D * D,
            moved=4 << 20,
        )(state, other, table, w_self)
        query, cross_query = call(
            query_body,
            (shape((tokens, HALF), BF16),) * 2,
            (vm, vm, vm, pl.ANY),
            scratch=(vm((D, HALF), BF16), pltpu.SemaphoreType.DMA),
            flops=2 * tokens * D * D,
            moved=4 << 20,
        )(mixed, plain, w_self, w_cross)
        side_a = exchanged(pair, "seq", 1, True)
        side_b = exchanged(pair, "seq", 1, False)
        tail_a = exchanged(tail, "seq", ROW, True)
        if step == 0:
            guide_rows = every_guide(guidance, cycle_size)
        guide_pair = call(
            functools.partial(guide_body, step, guidance.shape[1]),
            shape((every, D), BF16),
            (vm, vm),
            flops=2 * every * D * D,
            moved=3 << 20,
        )(guide_rows, w_cross)
        row_pairs = []
        for half in (row_a, row_b):
            row_pairs.append(
                call(
                    away_body,
                    shape((half.shape[0], D), BF16),
                    (vm, vm, vm, vm),
                    flops=2 * half.shape[0] * D * D,
                    moved=4 << 20,
                )(half, partner_swap(half, "head", 1), table, w_self)
            )
        guided = call(
            cross_body,
            shape((tokens, HALF), BF16),
            (vm, vm),
            scratch=(vm((2, every // BLOCK, 2 * BLOCK, BLOCK), F32),),
            flops=8 * tokens * every * HALF,
            moved=1 << 20,
        )(cross_query, guide_pair)
        blocks = tokens // BLOCK
        out_weights = (self_out_weight, cross_out_weight)
        window, attended, received = None, [], []
        for block in range(blocks):
            outs = (shape((BLOCK, HALF), BF16),) * 2
            if block == 0:
                outs = outs + (shape((5 * blocks, BLOCK, D), BF16),)
                tiles = (pair, side_a, side_b, row_pairs[0], tail_a, row_pairs[1])
                body = first_block_body
            else:
                tiles = (window,)
                body = functools.partial(later_block_body, block)
            operands = (block_lists, query, *tiles, guided, table, *out_weights)
            send, mine, *rest = call(
                body,
                outs,
                (sm,) + (vm,) * (len(operands) - 1),
                scratch=(vm((2, MAXK, 2 * BLOCK, BLOCK), F32),),
                flops=8 * BLOCK * MAXK * BLOCK * HALF + 4 * BLOCK * HALF * HALF,
                moved=4 << 20,
            )(*operands)
            window = rest[0] if rest else window
            attended.append(mine)
            received.append(partner_swap(send, "head", 1))
        base = call(
            base_body,
            shape((tokens, HALF), F32),
            (vm,) * (8 + blocks),
            flops=4 * tokens * HALF * HALF,
            moved=4 << 20,
        )(guided, table, *out_weights, state, known, latents, seam, *attended)
        last = step == STEPS - 1
        state, *heads = call(
            functools.partial(finish_body, blocks),
            (shape((tokens, HALF), BF16),)
            + (() if last else (shape((tokens // 2, HALF), BF16),)),
            (vm,) * (3 + blocks),
            flops=4 * tokens * HALF,
            moved=1 << 20,
        )(base, seam, table, *received)
        head = heads[0] if heads else None
    return state


def solution(mesh):
    in_specs = (
        P("seq", "head"),
        P("seq", "head"),
        P("seq"),
        P(),
        P("seq", None),
        P(None, "seq", None),
        P(),
        P(None, None, "head"),
        P("head", None),
        P(None, None, "head"),
        P("head", None),
    )
    out_specs = P("seq", "head")
    return jax.shard_map(
        on_device, mesh=mesh, in_specs=in_specs, out_specs=out_specs, check_vma=False
    )
```

```python
import functools
import math

import jax
import jax.numpy as jnp
from jax import lax
from jax.experimental import pallas as pl
from jax.experimental.pallas import tpu as pltpu
from jax.sharding import PartitionSpec as P


D = 1024
HEAD_DIM = 64
FREQ = 256
BLOCK = 128
MAXK = 6
ROW = 4
STEPS = 2
LANES = 128
HALF = D // 2
F32 = jnp.float32
BF16 = jnp.bfloat16
VMEM_LIMIT = 16 * 1024 * 1024


def pairing(size, stride, first):
    route = []
    for i in range(size):
        even = (i // stride) % 2 == 0
        route.append((i, (i + (stride if even == first else -stride)) % size))
    return route


def exchanged(block, axis, stride, first):
    return lax.ppermute(block, axis, pairing(lax.axis_size(axis), stride, first))


def partner_swap(block, axis, mask):
    return lax.ppermute(block, axis, [(i ^ mask, i) for i in range(lax.axis_size(axis))])


def table_body(times_ref, weight_ref, latent_hbm, known_hbm, *refs):
    table_refs = refs[:STEPS]
    latent_ref, known_ref, latent_sem, known_sem = refs[STEPS:]
    latent_copy = pltpu.make_async_copy(latent_hbm, latent_ref, latent_sem)
    known_copy = pltpu.make_async_copy(known_hbm, known_ref, known_sem)
    latent_copy.start()
    known_copy.start()
    half = FREQ // 2
    row = lax.broadcasted_iota(jnp.int32, (8, LANES), 0)
    column = lax.broadcasted_iota(jnp.int32, (8, half), 1).astype(F32)
    moments = jnp.zeros((8, LANES), F32)
    for index in range(STEPS + 1):
        moments = jnp.where(row == index, times_ref[index].astype(F32), moments)
    phase = moments * jnp.exp(-math.log(10000.0) * column / half)
    cosine, sine = jnp.cos(phase), jnp.sin(phase)
    cosine = (cosine * jax.nn.sigmoid(cosine)).astype(BF16)
    sine = (sine * jax.nn.sigmoid(sine)).astype(BF16)
    for part in range(weight_ref.shape[0]):
        rows = jnp.dot(cosine, weight_ref[part, :half, :], preferred_element_type=F32)
        rows = rows + jnp.dot(sine, weight_ref[part, half:, :], preferred_element_type=F32)
        for step, table_ref in enumerate(table_refs):
            table_ref[part : part + 1, :] = rows[step : step + 1]
    level = jnp.cos((moments / 1000.0 + 0.008) / 1.008 * (math.pi / 2.0))
    level = level * level
    root, rest = jnp.sqrt(level), jnp.sqrt(1.0 - level)
    for step, table_ref in enumerate(table_refs):
        root_after, rest_after = root[step + 1 : step + 2, :1], rest[step + 1 : step + 2, :1]
        ratio = root_after / root[step : step + 1, :1]
        gain = rest_after - ratio * rest[step : step + 1, :1]
        for place, value in enumerate((ratio, gain, root_after, rest_after)):
            table_ref[4 + place : 5 + place, :] = jnp.broadcast_to(value, (1, D))
    latent_copy.wait()
    known_copy.wait()


def call(body, out, ins, scratch=(), flops=0, moved=0):
    return pl.pallas_call(
        body,
        out_shape=out,
        in_specs=[pl.BlockSpec(memory_space=m) for m in ins],
        out_specs=jax.tree.map(lambda _: pl.BlockSpec(memory_space=pltpu.VMEM), out),
        scratch_shapes=list(scratch),
        compiler_params=pltpu.CompilerParams(vmem_limit_bytes=VMEM_LIMIT),
        cost_estimate=pl.CostEstimate(flops=flops, bytes_accessed=moved, transcendentals=0),
    )


def halves():
    h = lax.axis_index("head")
    near = pl.ds(pl.multiple_of(h * HALF, HALF), HALF)
    far = pl.ds(pl.multiple_of((1 - h) * HALF, HALF), HALF)
    return near, far


def normalize(near, far):
    near = near.astype(F32)
    far = far.astype(F32)
    width = near.shape[1] + far.shape[1]
    mean = (
        jnp.sum(near, axis=1, keepdims=True) + jnp.sum(far, axis=1, keepdims=True)
    ) / width
    near = near - mean
    far = far - mean
    second = (
        jnp.sum(near * near, axis=1, keepdims=True) + jnp.sum(far * far, axis=1, keepdims=True)
    ) / width
    gain = lax.rsqrt(second + 1e-06)
    return near * gain, far * gain


def modulate(normed, table_ref, side):
    return (normed * (1.0 + table_ref[1:2, side]) + table_ref[0:1, side]).astype(BF16)


def two_dots(a, b, weight_ref, near, far, lead=None):
    if lead is None:
        wa, wb = weight_ref[near, :], weight_ref[far, :]
    else:
        wa, wb = weight_ref[lead, near, :], weight_ref[lead, far, :]
    return jnp.dot(a, wa, preferred_element_type=F32) + jnp.dot(b, wb, preferred_element_type=F32)


def own_body(near_ref, far_ref, table_ref, w_ref, kv_ref, tail_ref, mixed_ref, plain_ref):
    near, far = halves()
    na, nb = normalize(near_ref[...], far_ref[...])
    ma, mb = modulate(na, table_ref, near), modulate(nb, table_ref, far)
    kv_ref[:, :HALF] = two_dots(ma, mb, w_ref, near, far, 1).astype(BF16)
    kv_ref[:, HALF:] = two_dots(ma, mb, w_ref, near, far, 2).astype(BF16)
    tail_ref[...] = kv_ref[kv_ref.shape[0] - tail_ref.shape[0] :, :]
    mixed_ref[:, :HALF], mixed_ref[:, HALF:] = ma, mb
    plain_ref[:, :HALF], plain_ref[:, HALF:] = na.astype(BF16), nb.astype(BF16)


def query_body(mixed_ref, plain_ref, w_ref, cross_ref, q_ref, cq_ref, cw_ref, sem):
    fetch = pltpu.make_async_copy(cross_ref.at[0], cw_ref, sem)
    fetch.start()
    near, far = halves()
    scale = math.log2(math.e) / math.sqrt(HEAD_DIM)
    query = two_dots(mixed_ref[:, :HALF], mixed_ref[:, HALF:], w_ref, near, far, 0)
    q_ref[...] = (query * scale).astype(BF16)
    fetch.wait()
    query = two_dots(plain_ref[:, :HALF], plain_ref[:, HALF:], cw_ref, near, far)
    cq_ref[...] = (query * scale).astype(BF16)


def away_body(near_ref, far_ref, table_ref, w_ref, kv_ref):
    near, far = halves()
    na, nb = normalize(near_ref[...], far_ref[...])
    ma, mb = modulate(na, table_ref, near), modulate(nb, table_ref, far)
    kv_ref[:, :HALF] = two_dots(ma, mb, w_ref, near, far, 1).astype(BF16)
    kv_ref[:, HALF:] = two_dots(ma, mb, w_ref, near, far, 2).astype(BF16)


def guide_body(step, each, rows_ref, cw_ref, kv_ref):
    rows = rows_ref[...].astype(F32).reshape(-1, STEPS, each, D)[:, step].reshape(-1, D)
    center = rows - jnp.mean(rows, axis=1, keepdims=True)
    second = jnp.mean(center * center, axis=1, keepdims=True)
    plain = (center * lax.rsqrt(second + 1e-06)).astype(BF16)
    for part in range(2):
        both = jnp.dot(plain, cw_ref[part + 1], preferred_element_type=F32)
        kv_ref[:, part * HALF : (part + 1) * HALF] = both.astype(BF16)


def join_body(kept_ref, received_ref, out_ref):
    count = kept_ref.shape[0]
    out_ref[:count, :] = kept_ref[...]
    out_ref[count:, :] = received_ref[...]


def pair_scores(query, keys, live, held):
    rows = query.shape[0]
    low = lax.broadcasted_iota(jnp.int32, (rows, LANES), 1) < HEAD_DIM
    zero = jnp.zeros_like(query)
    stacked = jnp.concatenate([jnp.where(low, query, zero), jnp.where(low, zero, query)], axis=0)
    peak = None
    for index, key in enumerate(keys):
        score = lax.dot_general(
            stacked, key, (((1,), (1,)), ((), ())), preferred_element_type=F32
        )
        if live is not None and live[index] is not None:
            score = jnp.where(live[index], score, -1e30)
        held[index] = score
        peak = score if peak is None else jnp.maximum(peak, score)
    return jnp.max(peak, axis=1, keepdims=True)


def pair_mixed(peak, values, held):
    rows = held.shape[1] // 2
    low = lax.broadcasted_iota(jnp.int32, (rows, LANES), 1) < HEAD_DIM
    total, mixed = None, None
    for index, value in enumerate(values):
        weight = jnp.exp2(held[index] - peak)
        part = jnp.dot(weight.astype(BF16), value, preferred_element_type=F32)
        total = weight if total is None else total + weight
        mixed = part if mixed is None else mixed + part
    total = jnp.sum(total, axis=1, keepdims=True)
    chosen = jnp.where(low, mixed[:rows], mixed[rows:])
    return (chosen / jnp.where(low, total[:rows], total[rows:])).astype(BF16)


def attention(count, query_of, keys_of, values_of, live, held, store):
    peaks = [pair_scores(query_of(0), keys_of(0), live, held.at[0])]
    for pair in range(count):
        if pair + 1 < count:
            ahead = held.at[(pair + 1) % 2]
            peaks.append(pair_scores(query_of(pair + 1), keys_of(pair + 1), live, ahead))
        store(pair, pair_mixed(peaks[pair], values_of(pair), held.at[pair % 2]))


def cross_body(cq_ref, kv_ref, out_ref, held):
    count = kv_ref.shape[0]
    for block in range(cq_ref.shape[0] // BLOCK):
        at = pl.ds(block * BLOCK, BLOCK)

        def store(pair, value):
            out_ref[at, pl.ds(pair * LANES, LANES)] = value

        def columns(start):
            lanes = pl.ds(start, LANES)
            return [kv_ref[pl.ds(g, BLOCK), lanes] for g in range(0, count, BLOCK)]

        attention(
            HALF // LANES,
            lambda pair: cq_ref[at, pl.ds(pair * LANES, LANES)],
            lambda pair: columns(pair * LANES),
            lambda pair: columns(HALF + pair * LANES),
            None,
            held,
            store,
        )


def seam_column(seam_ref, block):
    shape = (BLOCK, BLOCK)
    same = lax.broadcasted_iota(jnp.int32, shape, 0) == lax.broadcasted_iota(jnp.int32, shape, 1)
    spread = jnp.broadcast_to(seam_ref[block : block + 1, :].astype(F32), shape)
    return jnp.sum(jnp.where(same, spread, 0.0), axis=1, keepdims=True) > 0.5


def first_block_body(list_ref, q_ref, *refs):
    tiles, (attended_ref, window, held) = refs[:-3], refs[-3:]
    filled = 0
    for tile in tiles:
        for block in range(tile.shape[0] // BLOCK):
            window[filled] = tile[pl.ds(block * BLOCK, BLOCK), :]
            filled += 1
    later_block_body(0, list_ref, q_ref, window, attended_ref, held)


def projected(attended_ref, guided, table_ref, wo_ref, wc_ref, side):
    first = jnp.dot(attended_ref[...], wo_ref[:, side], preferred_element_type=F32)
    second = jnp.dot(guided, wc_ref[:, side], preferred_element_type=F32)
    return table_ref[2:3, side] * first + table_ref[3:4, side] * second


def send_body(block, attended_ref, guided_ref, table_ref, wo_ref, wc_ref, send_ref):
    _, far = halves()
    guided = guided_ref[pl.ds(block * BLOCK, BLOCK), :]
    send_ref[...] = projected(attended_ref, guided, table_ref, wo_ref, wc_ref, far).astype(BF16)


def both_first_body(tiles, list_ref, q_ref, *refs):
    given, (send_ref, attended_ref, window, held) = refs[:-4], refs[-4:]
    first_block_body(list_ref, q_ref, *given[:tiles], attended_ref, window, held)
    send_body(0, attended_ref, *given[tiles:], send_ref)


def both_later_body(block, list_ref, q_ref, window, *refs):
    given, (send_ref, attended_ref, held) = refs[:-3], refs[-3:]
    later_block_body(block, list_ref, q_ref, window, attended_ref, held)
    send_body(block, attended_ref, *given, send_ref)


def later_block_body(block, list_ref, q_ref, window, attended_ref, held):
    per_tile = q_ref.shape[0] // BLOCK
    cycle = lax.axis_size("seq")
    position = lax.axis_index("seq")
    side_up = 1 + lax.rem(position, 2)
    row_up = 3 + lax.rem(lax.div(position, ROW), 2)
    at = pl.ds(block * BLOCK, BLOCK)
    live, picked = [], []
    for slot in range(MAXK):
        entry = list_ref[block, slot]
        tile = lax.div(jnp.maximum(entry, 0), per_tile)
        offset = tile - position
        offset = jnp.where(offset < 0, offset + cycle, offset)
        place = jnp.where(offset == ROW % cycle, row_up, 7 - row_up)
        place = jnp.where(offset == cycle - 1, 3 - side_up, place)
        place = jnp.where(offset == 1, side_up, place)
        place = jnp.where(jnp.logical_or(offset == 0, entry < 0), 0, place)
        live.append(None if slot == 0 else entry >= 0)
        picked.append(place * per_tile + lax.rem(jnp.maximum(entry, 0), per_tile))

    def store(pair, value):
        attended_ref[:, pl.ds(pair * LANES, LANES)] = value

    def columns(start):
        return [window[entry, :, pl.ds(start, LANES)] for entry in picked]

    attention(
        HALF // LANES,
        lambda pair: q_ref[at, pl.ds(pair * LANES, LANES)],
        lambda pair: columns(pair * LANES),
        lambda pair: columns(HALF + pair * LANES),
        live,
        held,
        store,
    )


def base_body(
    guided_ref, table_ref, wo_ref, wc_ref, state_ref, known_ref, latent_ref, seam_ref, *refs
):
    near, _ = halves()
    ratio, gain = table_ref[4:5, :HALF], table_ref[5:6, :HALF]
    root_after, rest_after = table_ref[6:7, :HALF], table_ref[7:8, :HALF]
    base_ref = refs[-1]
    for block, attended_ref in enumerate(refs[:-1]):
        rows = slice(block * BLOCK, (block + 1) * BLOCK)
        kept_part = projected(attended_ref, guided_ref[rows, :], table_ref, wo_ref, wc_ref, near)
        moved = ratio * state_ref[rows, :].astype(F32) + gain * kept_part
        kept = root_after * known_ref[rows, :].astype(F32)
        kept = kept + rest_after * latent_ref[rows, :].astype(F32)
        base_ref[rows, :] = jnp.where(seam_column(seam_ref, block), moved, kept)


def finish_body(blocks, base_ref, seam_ref, table_ref, *refs):
    gain = table_ref[5:6, :HALF]
    state_ref = refs[blocks]
    for block, received_ref in enumerate(refs[:blocks]):
        rows = slice(block * BLOCK, (block + 1) * BLOCK)
        base = base_ref[rows, :]
        moved = base + gain * received_ref[...].astype(F32)
        state_ref[rows, :] = jnp.where(seam_column(seam_ref, block), moved, base).astype(BF16)
    for head_ref in refs[blocks + 1 :]:
        head_ref[...] = state_ref[: head_ref.shape[0], :]


def every_guide(guidance, cycle_size):
    steps, count, width = guidance.shape
    rows = guidance.reshape(steps * count, width)
    bits = cycle_size.bit_length() - 1
    for bit in (*range(2, bits), 1, 0):
        received = partner_swap(rows, "seq", 1 << bit)
        rows = call(
            join_body,
            jax.ShapeDtypeStruct((2 * rows.shape[0], width), BF16),
            (pltpu.VMEM, pltpu.VMEM),
            moved=rows.size * 4,
        )(rows, received)
    return rows


def cross_attention(query, guide_pair):
    tokens, every = query.shape[0], guide_pair.shape[0]
    return call(
        cross_body,
        jax.ShapeDtypeStruct((tokens, HALF), BF16),
        (pltpu.VMEM,) * 2,
        scratch=(pltpu.VMEM((2, every // BLOCK, 2 * BLOCK, BLOCK), F32),),
        flops=8 * tokens * every * HALF,
        moved=1 << 20,
    )(query, guide_pair)


def on_device(
    latents,
    known,
    seam_mask,
    timesteps,
    block_lists,
    guidance,
    modulation_weight,
    self_weight,
    self_out_weight,
    cross_weight,
    cross_out_weight,
):
    cycle_size = lax.axis_size("seq")
    tokens = latents.shape[0]
    vm, sm = pltpu.VMEM, pltpu.SMEM
    shape = jax.ShapeDtypeStruct
    every = cycle_size * guidance.shape[1]

    w_self = jnp.transpose(self_weight, (1, 0, 2))
    w_cross = jnp.transpose(cross_weight, (1, 0, 2))
    seam = seam_mask.reshape(tokens // BLOCK, BLOCK)
    state, head = latents, latents[: tokens // 2]
    for step in range(STEPS):
        other = partner_swap(state, "head", 1)
        row_b = exchanged(state, "seq", ROW, False)
        row_a = exchanged(head, "seq", ROW, True)
        if step == 0:
            *tables, latents, known = call(
                table_body,
                (shape((8, D), F32),) * STEPS + (shape((tokens, HALF), BF16),) * 2,
                (sm, vm, pl.ANY, pl.ANY),
                scratch=(pltpu.SemaphoreType.DMA,) * 2,
                flops=16 * FREQ * 4 * D,
                moved=2 << 20,
            )(timesteps, jnp.transpose(modulation_weight, (1, 0, 2)), latents, known)
            state = latents
        table = tables[step]
        pair, tail, mixed, plain = call(
            own_body,
            (
                shape((tokens, D), BF16),
                shape((tokens // 2, D), BF16),
                shape((tokens, D), BF16),
                shape((tokens, D), BF16),
            ),
            (vm, vm, vm, vm),
            flops=2 * tokens * D * D,
            moved=4 << 20,
        )(state, other, table, w_self)
        query, cross_query = call(
            query_body,
            (shape((tokens, HALF), BF16),) * 2,
            (vm, vm, vm, pl.ANY),
            scratch=(vm((D, HALF), BF16), pltpu.SemaphoreType.DMA),
            flops=2 * tokens * D * D,
            moved=4 << 20,
        )(mixed, plain, w_self, w_cross)
        side_a = exchanged(pair, "seq", 1, True)
        side_b = exchanged(pair, "seq", 1, False)
        tail_a = exchanged(tail, "seq", ROW, True)
        if step == 0:
            guide_rows = every_guide(guidance, cycle_size)
        guide_pair = call(
            functools.partial(guide_body, step, guidance.shape[1]),
            shape((every, D), BF16),
            (vm, vm),
            flops=2 * every * D * D,
            moved=3 << 20,
        )(guide_rows, w_cross)
        row_pairs = []
        for half in (row_a, row_b):
            row_pairs.append(
                call(
                    away_body,
                    shape((half.shape[0], D), BF16),
                    (vm, vm, vm, vm),
                    flops=2 * half.shape[0] * D * D,
                    moved=4 << 20,
                )(half, partner_swap(half, "head", 1), table, w_self)
            )
        blocks = tokens // BLOCK
        out_weights = (self_out_weight, cross_out_weight)
        early = step == 0
        if not early:
            guided = cross_attention(cross_query, guide_pair)
        tiles = (pair, side_a, side_b, row_pairs[0], tail_a, row_pairs[1])
        block_shape = shape((BLOCK, HALF), BF16)
        attended, received = [], []
        for block in range(blocks):
            outs = (block_shape,) if early else (block_shape,) * 2
            if block == 0:
                outs = outs + (shape((5 * blocks, BLOCK, D), BF16),)
                given = tiles
                body = first_block_body
                if not early:
                    body = functools.partial(both_first_body, len(tiles))
            else:
                given = (window,)
                body = later_block_body if early else both_later_body
                body = functools.partial(body, block)
            if not early:
                given = (*given, guided, table, *out_weights)
            got = call(
                body,
                outs,
                (sm,) + (vm,) * (1 + len(given)),
                scratch=(vm((2, MAXK, 2 * BLOCK, BLOCK), F32),),
                flops=8 * BLOCK * MAXK * BLOCK * HALF + 4 * BLOCK * HALF * HALF,
                moved=4 << 20,
            )(block_lists, query, *given)
            got = list(got)
            if block == 0:
                window = got.pop()
            attended.append(got.pop())
            if not early:
                received.append(partner_swap(got.pop(), "head", 1))
        if early:
            guided = cross_attention(cross_query, guide_pair)
            for block in range(blocks):
                send = call(
                    functools.partial(send_body, block),
                    block_shape,
                    (vm,) * 5,
                    flops=4 * BLOCK * HALF * HALF,
                    moved=2 << 20,
                )(attended[block], guided, table, *out_weights)
                received.append(partner_swap(send, "head", 1))
        base = call(
            base_body,
            shape((tokens, HALF), F32),
            (vm,) * (8 + blocks),
            flops=4 * tokens * HALF * HALF,
            moved=4 << 20,
        )(guided, table, *out_weights, state, known, latents, seam, *attended)
        last = step == STEPS - 1
        state, *heads = call(
            functools.partial(finish_body, blocks),
            (shape((tokens, HALF), BF16),)
            + (() if last else (shape((tokens // 2, HALF), BF16),)),
            (vm,) * (3 + blocks),
            flops=4 * tokens * HALF,
            moved=1 << 20,
        )(base, seam, table, *received)
        head = heads[0] if heads else None
    return state


def solution(mesh):
    in_specs = (
        P("seq", "head"),
        P("seq", "head"),
        P("seq"),
        P(),
        P("seq", None),
        P(None, "seq", None),
        P(),
        P(None, None, "head"),
        P("head", None),
        P(None, None, "head"),
        P("head", None),
    )
    out_specs = P("seq", "head")
    return jax.shard_map(
        on_device, mesh=mesh, in_specs=in_specs, out_specs=out_specs, check_vma=False
    )
```
